256 devices in a mesh: bits: 64 (over x, z_hi, y, core), freq: 4 (over z_lo).
Axes of the slice: x: 4, y: 4, z: 8 (z_hi: 2, z_lo: 4; z = z_hi * 4 + z_lo), core: 2. Of those that a mesh axis runs over, the one named last changes fastest.
Arguments:
- estimate: float32 [32768, 512], P('bits'), may hold values from -6 to 6
- observed: float32 [4, 32768, 512], P('freq', 'bits'), may hold values from -6 to 6
- factors: float32 [4, 4, 2, 32768, 256], P('freq', None, None, 'bits'), may hold values from -0.25 to 0.25
Outputs:
- updated: float32 [32768, 512], P('bits')
The draws below stay inside these ranges and needn't reach their ends.
All inputs are finite; a program needn't handle non-finite values.
Results may differ from the reference program's by a relative error of at most 0.00015.
Values sent between devices are 32-bit elements; how exact they have to be, the bound alone decides.
No kernel may reach another device: no remote copies, remote signals or barrier semaphores. Data moves between devices by JAX's collectives and lax.ppermute only.
A program may use at most 64 MiB of HBM per device.

```python
import jax
import jax.numpy as jnp
import numpy as np
from jax import lax

TILE = 256
BLK = 2
SOURCES = 512
LEVELS = 4
FREQS = 4
M = 32768
N_BITS = 64


def shard_levels(stream_key, shape, cuts, smallest, top_value):
    def one(position, parts):
        heights = jax.random.uniform(jax.random.fold_in(jax.random.fold_in(stream_key, 6), position), (parts,), jnp.float32, smallest / len(cuts), top_value / len(cuts))
        return jnp.repeat(jnp.exp(heights), shape[position] // parts).reshape((-1,) + (1,) * (len(shape) - position - 1))

    gain = one(*cuts[0])
    for cut in cuts[1:]:
        gain = gain * one(*cut)
    return gain


def gaussian(key, shape, scale, most, cuts=(), held_as=jnp.bfloat16):
    array = scale * jax.random.normal(key, shape, jnp.float32)
    if cuts:
        array = array * shard_levels(key, shape, cuts, -0.22, 0.18)
    return jnp.clip(array, -most, most).astype(held_as)


def setup_inputs(seed: int = 0) -> dict:
    keys = jax.random.split(jax.random.key(seed), 4)
    return {
        "estimate": gaussian(keys[0], (M, SOURCES), 1.0, 6.0, ((0, 64),), jnp.float32),
        "observed": gaussian(keys[1], (FREQS, M, SOURCES), 1.0, 6.0, ((0, 4), (1, 64)), jnp.float32),
        "factors": gaussian(keys[2], (FREQS, LEVELS, 2, M, TILE), (2 * TILE) ** -0.5, 0.25, ((0, 4), (3, 64)), jnp.float32),
    }


def apply_tile(tile_set, field):
    return jnp.einsum("nbij,nbjs->nbis", tile_set, field, precision=lax.Precision.HIGHEST)


def apply_transposed(tile_set, field):
    return jnp.einsum("nbji,nbjs->nbis", tile_set, field, precision=lax.Precision.HIGHEST)


def reference(estimate, observed, factors):
    bit_count = N_BITS.bit_length() - 1
    device_ids = np.arange(N_BITS)
    start = estimate.reshape(N_BITS, BLK, TILE, SOURCES)
    total = jnp.zeros_like(start)
    for freq_index in range(FREQS):
        shaped = factors[freq_index].reshape(LEVELS, 2, N_BITS, BLK, TILE, TILE)
        current = start
        for level_index in range(LEVELS):
            bit_index = (bit_count - 1 - level_index) % bit_count
            partner_index = device_ids ^ (1 << bit_index)
            partner_field = current[partner_index]
            current = apply_tile(shaped[level_index, 0], current) + apply_tile(shaped[level_index, 1], partner_field)
        adjoint = observed[freq_index].reshape(N_BITS, BLK, TILE, SOURCES) - current
        for level_index in reversed(range(LEVELS)):
            bit_index = (bit_count - 1 - level_index) % bit_count
            partner_index = device_ids ^ (1 << bit_index)
            sent_terms = apply_transposed(shaped[level_index, 1], adjoint)
            adjoint = apply_transposed(shaped[level_index, 0], adjoint) + sent_terms[partner_index]
        total = total + adjoint
    return (start + total).reshape(M, SOURCES)
```

```python
import jax
import jax.numpy as jnp
from jax import lax
from jax.sharding import PartitionSpec as P

COLUMN_CUTS = 2


def flip(value, axis, mask):
    pairs = [(source, source ^ mask) for source in range(lax.axis_size(axis))]
    return lax.ppermute(value, axis, pairs)


def times(tile, field):
    return jnp.dot(tile, field, precision=lax.Precision.HIGH)


def times_transposed(tile, field):
    return lax.dot_general(tile, field, (((0,), (0,)), ((), ())), precision=lax.Precision.HIGH)


def local(estimate, observed, factors):
    bit_count = lax.axis_size("bits").bit_length() - 1
    levels = factors.shape[1]
    width = factors.shape[-1]
    blocks = estimate.shape[0] // width
    sources = estimate.shape[1]
    cols = sources // COLUMN_CUTS
    masks = [1 << ((bit_count - 1 - level) % bit_count) for level in range(levels)]
    place = lax.axis_index("freq")
    results = {}
    for j in range(blocks):
        rows = slice(j * width, (j + 1) * width)
        for cut in range(COLUMN_CUTS):
            span = slice(cut * cols, (cut + 1) * cols)
            first = estimate[rows, span]
            current = first
            for level in range(levels):
                other = flip(current, "bits", masks[level])
                current = times(factors[0, level, 0, rows], current) + times(factors[0, level, 1, rows], other)
            adjoint = observed[0, rows, span] - current
            for level in reversed(range(levels)):
                arrived = flip(times_transposed(factors[0, level, 1, rows], adjoint), "bits", masks[level])
                adjoint = times_transposed(factors[0, level, 0, rows], adjoint) + arrived
            half = width // 2
            odd = place % 2 == 1
            low, high = adjoint[:half], adjoint[half:]
            kept = jnp.where(odd, high, low)
            kept = kept + flip(jnp.where(odd, low, high), "freq", 1)
            quarter = half // 2
            upper = place // 2 == 1
            low, high = kept[:quarter], kept[quarter:]
            mine = jnp.where(upper, high, low)
            mine = mine + flip(jnp.where(upper, low, high), "freq", 2)
            theirs = flip(mine, "freq", 2)
            kept = jnp.concatenate([jnp.where(upper, theirs, mine), jnp.where(upper, mine, theirs)])
            theirs = flip(kept, "freq", 1)
            total = jnp.concatenate([jnp.where(odd, theirs, kept), jnp.where(odd, kept, theirs)])
            results[j, cut] = first + total
    return jnp.concatenate(
        [jnp.concatenate([results[j, cut] for cut in range(COLUMN_CUTS)], axis=1) for j in range(blocks)], axis=0
    )


def solution(mesh):
    in_specs = (P("bits", None), P("freq", "bits", None), P("freq", None, None, "bits", None))
    out_specs = P("bits", None)
    return jax.shard_map(local, mesh=mesh, in_specs=in_specs, out_specs=out_specs, check_vma=False)
```

```python
import functools
import jax
import jax.numpy as jnp
from jax import lax
from jax.experimental import pallas as pl
from jax.experimental.pallas import tpu as pltpu
from jax.sharding import PartitionSpec as P


CHUNKS = [(0, 0, 128), (1, 0, 256), (0, 128, 256), (1, 256, 256), (0, 384, 128)]
FIRST_GROUPS = [[0], [1], [2], [3], [4]]
SUM_GROUPS = [[0], [1], [2], [3], [4]]
ORDER = (
    "X0 X1 A1 B1",
    "A2 X2 B2 C1",
    "A3 X4 X3 C2",
    "E1 B3 A4 D1",
    "E2 B4 D2 C3",
    "E3 B5 C4 D3",
    "C5 D4 B6 A5",
    "E4 B7 D5 C6",
    "P1.8 A6 C7 E5",
    "D6 A7 P1.9 P2.8",
    "D7 P1.10 P0.8 E6",
    "P2.9 P3.8 E7 P0.9",
    "P2.10 P3.9 P4.8 P0.10",
    "P4.9 P3.10 P4.10",
)
EVENTS = " ".join(ORDER).split()
ANY = pl.BlockSpec(memory_space=pl.ANY)
VM = pl.BlockSpec(memory_space=pltpu.VMEM)
PARAMS = pltpu.CompilerParams(vmem_limit_bytes=8 << 20)
FORWARD = ((1,), (0,))
BACKWARD = ((0,), (0,))


def split(value):
    high = value.astype(jnp.bfloat16)
    return high, (value - high.astype(jnp.float32)).astype(jnp.bfloat16)


def product(tile, field, dims):
    (a, b), (c, d) = tile, field
    dot = functools.partial(lax.dot_general, dimension_numbers=(dims, ((), ())), preferred_element_type=jnp.float32)
    return dot(a, c) + (dot(a, d) + dot(b, c))


def tiles_of(ref):
    return (ref[0, 0], ref[0, 1]), (ref[1, 0], ref[1, 1])


def prepare_kernel(tiles_ref, *out_refs):
    levels, width = tiles_ref.shape[0], tiles_ref.shape[-1]
    blocks = len(out_refs) // levels
    for level in range(levels):
        for block in range(blocks):
            for which in range(2):
                high, low = split(tiles_ref[level, which, block * width:(block + 1) * width])
                out_refs[level * blocks + block][which, 0] = high
                out_refs[level * blocks + block][which, 1] = low


def forward_kernel(v_at, u_at, tiles_ref, v_ref, u_ref, token_ref, out_ref):
    own, other = tiles_of(tiles_ref)
    out_ref[...] = product(own, split(v_ref[v_at]), FORWARD) + product(other, split(u_ref[u_at]), FORWARD)


def turn_kernel(at, tiles_ref, v_ref, u_ref, seen_ref, token_ref, kept_ref, sent_ref):
    own, other = tiles_of(tiles_ref)
    predicted = product(own, split(v_ref[...]), FORWARD) + product(other, split(u_ref[...]), FORWARD)
    residual = split(seen_ref[at] - predicted)
    sent_ref[...] = product(other, residual, BACKWARD)
    kept_ref[...] = product(own, residual, BACKWARD)


def backward_kernel(tiles_ref, k_ref, a_ref, token_ref, kept_ref, sent_ref):
    own, other = tiles_of(tiles_ref)
    total = split(k_ref[...] + a_ref[...])
    sent_ref[...] = product(other, total, BACKWARD)
    kept_ref[...] = product(own, total, BACKWARD)


def join_kernel(count, *refs):
    out_ref = refs[-1]
    at = 0
    for k_ref, a_ref in zip(refs[:count], refs[count:2 * count]):
        cols = k_ref.shape[1]
        out_ref[:, at:at + cols] = k_ref[...] + a_ref[...]
        at += cols


def add_kernel(a_ref, b_ref, token_ref, out_ref):
    out_ref[...] = a_ref[...] + b_ref[...]


def local(estimate, observed, factors):
    bit_count = lax.axis_size("bits").bit_length() - 1
    levels = factors.shape[1]
    width = factors.shape[-1]
    blocks = estimate.shape[0] // width
    place = lax.axis_index("freq")
    freqs = lax.axis_size("freq")
    edge = (place == 0) | (place == freqs - 1)
    observed = observed[0]

    def flip(value, level):
        mask = 1 << ((bit_count - 1 - level) % bit_count)
        pairs = [(source, source ^ mask) for source in range(lax.axis_size("bits"))]
        return lax.ppermute(value, "bits", pairs)

    def call(kernel, ins, shapes, flops):
        outs = [jax.ShapeDtypeStruct(shape, jnp.float32) for shape in shapes]
        single = len(outs) == 1
        return pl.pallas_call(
            kernel,
            in_specs=[VM] * (len(ins) - 1) + [ANY],
            out_specs=VM if single else [VM] * len(outs),
            out_shape=outs[0] if single else outs,
            compiler_params=PARAMS,
            cost_estimate=pl.CostEstimate(flops=flops, bytes_accessed=4 * width * width * 4, transcendentals=0),
        )(*ins)

    prepared = pl.pallas_call(
        prepare_kernel,
        in_specs=[VM],
        out_specs=[VM] * (levels * blocks),
        out_shape=[jax.ShapeDtypeStruct((2, 2, width, width), jnp.bfloat16)] * (levels * blocks),
        name="prepare",
        compiler_params=pltpu.CompilerParams(vmem_limit_bytes=24 << 20),
    )(factors[0])

    first_of, offset_of = {}, {}
    for group, members in enumerate(FIRST_GROUPS):
        for chunk in members:
            first_of[chunk] = group
            offset_of[chunk] = CHUNKS[chunk][1] - CHUNKS[members[0]][1]
    state, arrived, sums = {}, {}, {}
    token = estimate
    for event in EVENTS:
        if event[0] == "X":
            group = int(event[1:])
            members = FIRST_GROUPS[group]
            block, first, _ = CHUNKS[members[0]]
            cols = sum(CHUNKS[chunk][2] for chunk in members)
            arrived[group] = flip(estimate[block * width:(block + 1) * width, first:first + cols], 0)
        elif event[0] == "P":
            group, step = (int(part) for part in event[1:].split("."))
            members = SUM_GROUPS[group]
            cols = sum(CHUNKS[chunk][2] for chunk in members)
            shape = [(width, cols)]
            if step == 2 * levels:
                ins = [state[chunk][0] for chunk in members] + [state[chunk][1] for chunk in members] + [token]
                total = call(functools.partial(join_kernel, len(members)), ins, shape, 1000)
            else:
                total = call(add_kernel, [*sums[group], token], shape, 1000)
            token = total
            pairs = [[(0, 1), (3, 2)], [(1, 2), (2, 1)], [(1, 0), (2, 3)]][step - 2 * levels]
            sums[group] = (total, lax.ppermute(total, "freq", pairs))
        else:
            chunk, step = ord(event[0]) - 65, int(event[1:])
            block, first, cols = CHUNKS[chunk]
            shape = (width, cols)
            flops = 12 * width * width * cols
            level = step - 1 if step <= levels else 2 * levels - 1 - step
            tile = prepared[level * blocks + block]
            rows = slice(block * width, (block + 1) * width)
            if step == 1:
                offset = offset_of[chunk]
                kernel = functools.partial(forward_kernel, (rows, slice(first, first + cols)), (slice(None), slice(offset, offset + cols)))
                token = call(kernel, [tile, estimate, arrived[first_of[chunk]], token], [shape], flops)
                state[chunk] = (token, flip(token, step))
            elif step < levels:
                kernel = functools.partial(forward_kernel, Ellipsis, Ellipsis)
                token = call(kernel, [tile, *state[chunk], token], [shape], flops)
                state[chunk] = (token, flip(token, step))
            elif step == levels:
                kernel = functools.partial(turn_kernel, (rows, slice(first, first + cols)))
                kept, sent = call(kernel, [tile, *state[chunk], observed, token], [shape] * 2, 2 * flops)
                token = kept
                state[chunk] = (kept, flip(sent, level))
            else:
                kept, sent = call(backward_kernel, [tile, *state[chunk], token], [shape] * 2, flops)
                token = kept
                state[chunk] = (kept, flip(sent, level))
    places = {}
    for group, members in enumerate(SUM_GROUPS):
        kept, came = sums[group]
        at = 0
        for chunk in members:
            cols = CHUNKS[chunk][2]
            places[CHUNKS[chunk][:2]] = jnp.where(edge, came[:, at:at + cols], kept[:, at:at + cols])
            at += cols
    rows = [
        jnp.concatenate([places[key] for key in sorted(places) if key[0] == block], axis=1) for block in range(blocks)
    ]
    return estimate + jnp.concatenate(rows, axis=0)


def solution(mesh):
    in_specs = (P("bits", None), P("freq", "bits", None), P("freq", None, None, "bits", None))
    out_specs = P("bits", None)

    return jax.shard_map(local, mesh=mesh, in_specs=in_specs, out_specs=out_specs, check_vma=False)
```

```python
import functools
import jax
import jax.numpy as jnp
from jax import lax
from jax.experimental import pallas as pl
from jax.experimental.pallas import tpu as pltpu
from jax.sharding import PartitionSpec as P


CHUNKS = [(0, 0, 256), (1, 0, 256), (0, 256, 256), (1, 256, 256)]
FIRST_GROUPS = [[0], [1], [2], [3]]
SUM_GROUPS = [[0], [1], [2], [3]]
ORDER = (
    "X0 X2 A1 X3",
    "C1 A2 X1 D1",
    "C2 B1 A3 D2",
    "A4 B2 C3 A5",
    "C4 D3 B3 C5",
    "D4 B4 A6 D5",
    "C6 B5 A7 C7",
    "D6 P0.8 B6 P0.9",
    "D7 P2.8 B7 P2.9",
    "P3.8 P1.8 P3.9 P2.10",
    "P1.9 P0.10 P3.10 P1.10",
)
EVENTS = " ".join(ORDER).split()
ANY = pl.BlockSpec(memory_space=pl.ANY)
SM = pl.BlockSpec(memory_space=pltpu.SMEM)
VM = pl.BlockSpec(memory_space=pltpu.VMEM)
PARAMS = pltpu.CompilerParams(vmem_limit_bytes=8 << 20)
FORWARD = ((1,), (0,))
BACKWARD = ((0,), (0,))


def split(value):
    high = value.astype(jnp.bfloat16)
    return high, (value - high.astype(jnp.float32)).astype(jnp.bfloat16)


def product(tile, field, dims):
    (a, b), (c, d) = tile, field
    dot = functools.partial(lax.dot_general, dimension_numbers=(dims, ((), ())), preferred_element_type=jnp.float32)
    return dot(a, c) + (dot(a, d) + dot(b, c))


def tiles_of(ref):
    return (ref[0, 0], ref[0, 1]), (ref[1, 0], ref[1, 1])


def prepare_kernel(tiles_ref, *out_refs):
    levels, width = tiles_ref.shape[0], tiles_ref.shape[-1]
    blocks = len(out_refs) // levels
    for level in range(levels):
        for block in range(blocks):
            for which in range(2):
                high, low = split(tiles_ref[level, which, block * width:(block + 1) * width])
                out_refs[level * blocks + block][which, 0] = high
                out_refs[level * blocks + block][which, 1] = low


def forward_kernel(v_at, u_at, tiles_ref, v_ref, u_ref, token_ref, out_ref):
    own, other = tiles_of(tiles_ref)
    out_ref[...] = product(own, split(v_ref[v_at]), FORWARD) + product(other, split(u_ref[u_at]), FORWARD)


def turn_kernel(at, tiles_ref, v_ref, u_ref, seen_ref, token_ref, kept_ref, sent_ref):
    own, other = tiles_of(tiles_ref)
    predicted = product(own, split(v_ref[...]), FORWARD) + product(other, split(u_ref[...]), FORWARD)
    residual = split(seen_ref[at] - predicted)
    sent_ref[...] = product(other, residual, BACKWARD)
    kept_ref[...] = product(own, residual, BACKWARD)


def backward_kernel(tiles_ref, k_ref, a_ref, token_ref, kept_ref, sent_ref):
    own, other = tiles_of(tiles_ref)
    total = split(k_ref[...] + a_ref[...])
    sent_ref[...] = product(other, total, BACKWARD)
    kept_ref[...] = product(own, total, BACKWARD)


def halve_kernel(count, place_ref, *refs):
    keep_ref, send_ref = refs[-2:]
    half = keep_ref.shape[0]
    odd = place_ref[0] % 2
    keep = pl.ds(pl.multiple_of(odd * half, half), half)
    send = pl.ds(pl.multiple_of((1 - odd) * half, half), half)
    at = 0
    for k_ref, a_ref in zip(refs[:count], refs[count:2 * count]):
        cols = k_ref.shape[1]
        keep_ref[:, at:at + cols] = k_ref[keep, :] + a_ref[keep, :]
        send_ref[:, at:at + cols] = k_ref[send, :] + a_ref[send, :]
        at += cols


def add_kernel(a_ref, b_ref, token_ref, out_ref):
    out_ref[...] = a_ref[...] + b_ref[...]


def local(estimate, observed, factors):
    bit_count = lax.axis_size("bits").bit_length() - 1
    levels = factors.shape[1]
    width = factors.shape[-1]
    blocks = estimate.shape[0] // width
    place = lax.axis_index("freq")
    freqs = lax.axis_size("freq")
    odd = place % 2 == 1
    place_array = jnp.full((1,), place, jnp.int32)
    observed = observed[0]

    def flip(value, level):
        mask = 1 << ((bit_count - 1 - level) % bit_count)
        pairs = [(source, source ^ mask) for source in range(lax.axis_size("bits"))]
        return lax.ppermute(value, "bits", pairs)

    def call(kernel, ins, shapes, flops, placed=False):
        outs = [jax.ShapeDtypeStruct(shape, jnp.float32) for shape in shapes]
        single = len(outs) == 1
        return pl.pallas_call(
            kernel,
            in_specs=[SM] * placed + [VM] * (len(ins) - 1 - placed) + [ANY],
            out_specs=VM if single else [VM] * len(outs),
            out_shape=outs[0] if single else outs,
            compiler_params=PARAMS,
            cost_estimate=pl.CostEstimate(flops=flops, bytes_accessed=4 * width * width * 4, transcendentals=0),
        )(*ins)

    prepared = pl.pallas_call(
        prepare_kernel,
        in_specs=[VM],
        out_specs=[VM] * (levels * blocks),
        out_shape=[jax.ShapeDtypeStruct((2, 2, width, width), jnp.bfloat16)] * (levels * blocks),
        name="prepare",
        compiler_params=pltpu.CompilerParams(vmem_limit_bytes=24 << 20),
    )(factors[0])

    first_of, offset_of = {}, {}
    for group, members in enumerate(FIRST_GROUPS):
        for chunk in members:
            first_of[chunk] = group
            offset_of[chunk] = CHUNKS[chunk][1] - CHUNKS[members[0]][1]
    state, arrived, sums = {}, {}, {}
    token = estimate
    for event in EVENTS:
        if event[0] == "X":
            group = int(event[1:])
            members = FIRST_GROUPS[group]
            block, first, _ = CHUNKS[members[0]]
            cols = sum(CHUNKS[chunk][2] for chunk in members)
            arrived[group] = flip(estimate[block * width:(block + 1) * width, first:first + cols], 0)
        elif event[0] == "P":
            group, step = (int(part) for part in event[1:].split("."))
            members = SUM_GROUPS[group]
            cols = sum(CHUNKS[chunk][2] for chunk in members)
            shape = (width // 2, cols)
            if step == 2 * levels:
                ins = [place_array, *(state[chunk][0] for chunk in members), *(state[chunk][1] for chunk in members), token]
                kernel = functools.partial(halve_kernel, len(members))
                kept, sent = call(kernel, ins, [shape] * 2, 1000, True)
            else:
                kept = sent = call(add_kernel, [*sums[group], token], [shape], 1000)
            token = kept
            mask = [1, 2, 1][step - 2 * levels]
            pairs = [(source, source ^ mask) for source in range(freqs)]
            sums[group] = (kept, lax.ppermute(sent, "freq", pairs))
        else:
            chunk, step = ord(event[0]) - 65, int(event[1:])
            block, first, cols = CHUNKS[chunk]
            shape = (width, cols)
            flops = 12 * width * width * cols
            level = step - 1 if step <= levels else 2 * levels - 1 - step
            tile = prepared[level * blocks + block]
            rows = slice(block * width, (block + 1) * width)
            if step == 1:
                offset = offset_of[chunk]
                kernel = functools.partial(forward_kernel, (rows, slice(first, first + cols)), (slice(None), slice(offset, offset + cols)))
                token = call(kernel, [tile, estimate, arrived[first_of[chunk]], token], [shape], flops)
                state[chunk] = (token, flip(token, step))
            elif step < levels:
                kernel = functools.partial(forward_kernel, Ellipsis, Ellipsis)
                token = call(kernel, [tile, *state[chunk], token], [shape], flops)
                state[chunk] = (token, flip(token, step))
            elif step == levels:
                kernel = functools.partial(turn_kernel, (rows, slice(first, first + cols)))
                kept, sent = call(kernel, [tile, *state[chunk], observed, token], [shape] * 2, 2 * flops)
                token = kept
                state[chunk] = (kept, flip(sent, level))
            else:
                kept, sent = call(backward_kernel, [tile, *state[chunk], token], [shape] * 2, flops)
                token = kept
                state[chunk] = (kept, flip(sent, level))
    places = {}
    for group, members in enumerate(SUM_GROUPS):
        kept, came = sums[group]
        total = jnp.concatenate([jnp.where(odd, came, kept), jnp.where(odd, kept, came)])
        at = 0
        for chunk in members:
            cols = CHUNKS[chunk][2]
            places[CHUNKS[chunk][:2]] = total[:, at:at + cols]
            at += cols
    rows = [
        jnp.concatenate([places[key] for key in sorted(places) if key[0] == block], axis=1) for block in range(blocks)
    ]
    return estimate + jnp.concatenate(rows, axis=0)


def solution(mesh):
    in_specs = (P("bits", None), P("freq", "bits", None), P("freq", None, None, "bits", None))
    out_specs = P("bits", None)

    return jax.shard_map(local, mesh=mesh, in_specs=in_specs, out_specs=out_specs, check_vma=False)
```
